32 devices in a mesh: seq: 8 (over z, x), fsdp: 4 (over y, core).
Axes of the slice: x: 2, y: 2, z: 4, core: 2. Of those that a mesh axis runs over, the one named last changes fastest.
Arguments:
- inputs: bfloat16 [3, 2048, 8192], P(None, 'seq', 'fsdp'), may hold values from -6 to 6
- grad_out: bfloat16 [2048, 8192], P('seq', 'fsdp'), may hold values from -6 to 6
- filters: bfloat16 [128, 8192], P('fsdp'), may hold values from -0.5 to 0.5
- short_weights: bfloat16 [3, 3, 8192], P(None, None, 'fsdp'), may hold values from -3.5 to 3.5
Outputs:
- grad_inputs: bfloat16 [3, 2048, 8192], P(None, 'seq', 'fsdp')
- grad_filters: float32 [128, 8192], P('fsdp')
- grad_short: float32 [3, 3, 8192], P(None, None, 'fsdp')
The draws below stay inside these ranges and needn't reach their ends.
All inputs are finite; a program needn't handle non-finite values.
Results may differ from the reference program's by a relative error of at most 0.0057.
Values may be sent and summed in bfloat16 or wider, within the bound.
No kernel may reach another device: no remote copies, remote signals or barrier semaphores. Data moves between devices by JAX's collectives and lax.ppermute only.
A program may use at most 64 MiB of HBM per device.

```python
import jax
import jax.numpy as jnp
from jax import lax

WIDTH = 8192
FILTER_LEN = 128
SHORT_LEN = 3
SEQ_LEN = 2048


def block_levels(stream_key, dims, pieces, low, high):
    def one(dim, shards_of):
        heights = jax.random.uniform(jax.random.fold_in(jax.random.fold_in(stream_key, 6), dim), (shards_of,), jnp.float32, low / len(pieces), high / len(pieces))
        return jnp.repeat(jnp.exp(heights), dims[dim] // shards_of).reshape((-1,) + (1,) * (len(dims) - dim - 1))

    gain = one(*pieces[0])
    for cut in pieces[1:]:
        gain = gain * one(*cut)
    return gain


def noise(key, shape, spread, bound, shards=(), kind=jnp.bfloat16):
    drawn = jax.random.normal(key, shape, jnp.float32) * spread
    if len(shards) > 0:
        drawn = block_levels(key, shape, shards, -0.22, 0.18) * drawn
    return jnp.clip(drawn, min=-bound, max=bound).astype(kind)


def setup_inputs(seed: int = 0) -> dict:
    seeds = jax.random.split(jax.random.key(seed), 5)
    inputs = noise(seeds[0], (3, SEQ_LEN, WIDTH), 1.0, 6.0, ((1, 8), (2, 4)))
    grad_out = noise(seeds[1], (SEQ_LEN, WIDTH), 1.0, 6.0, ((0, 8), (1, 4)))
    filters = noise(seeds[2], (FILTER_LEN, WIDTH), FILTER_LEN ** -0.5, 0.5, ((0, 4),))
    short_weights = noise(seeds[3], (3, SHORT_LEN, WIDTH), SHORT_LEN ** -0.5, 3.5, ((2, 4),))
    return {"inputs": inputs, "grad_out": grad_out, "filters": filters, "short_weights": short_weights}


def reference(inputs, grad_out, filters, short_weights):
    block = 512 if WIDTH % 512 == 0 else WIDTH
    blocks = WIDTH // block
    lag = SHORT_LEN - 1
    length = inputs.shape[1]
    fft_len = length + FILTER_LEN

    def causal(signal, kernel):
        spectrum = jnp.fft.rfft(signal, fft_len, axis=0) * jnp.fft.rfft(kernel, fft_len, axis=0)
        return jnp.fft.irfft(spectrum, fft_len, axis=0)[:length]

    def one_block(first_col):
        source = lax.dynamic_slice_in_dim(inputs, first_col, block, 2).astype(jnp.float32)
        upstream = lax.dynamic_slice_in_dim(grad_out, first_col, block, 1).astype(jnp.float32)
        taps = lax.dynamic_slice_in_dim(filters, first_col, block, 1).astype(jnp.float32)
        weights = lax.dynamic_slice_in_dim(short_weights, first_col, block, 2).astype(jnp.float32)
        padded = jnp.pad(source, ((0, 0), (lag, 0), (0, 0)))
        shorts = weights[:, 0][:, None, :] * padded[:, lag:lag + length]
        for offset in range(1, SHORT_LEN):
            shorts = shorts + weights[:, offset][:, None, :] * padded[:, lag - offset:lag - offset + length]
        mixed_low = (shorts[1] * shorts[2]).astype(jnp.bfloat16)
        mixed = lax.optimization_barrier(mixed_low).astype(jnp.float32)
        long_out = causal(mixed, taps)
        grad_q = (upstream * long_out).astype(jnp.bfloat16)
        grad_long_low = (upstream * shorts[0]).astype(jnp.bfloat16)
        grad_long = lax.optimization_barrier(grad_long_low).astype(jnp.float32)
        grad_mixed = causal(grad_long[::-1], taps)[::-1]
        grad_k = (grad_mixed * shorts[2]).astype(jnp.bfloat16)
        grad_v = (grad_mixed * shorts[1]).astype(jnp.bfloat16)
        grads = lax.optimization_barrier(jnp.stack([grad_q, grad_k, grad_v])).astype(jnp.float32)
        trailing = jnp.pad(grads, ((0, 0), (0, lag), (0, 0)))
        grad_block = weights[:, 0][:, None, :] * trailing[:, 0:length]
        for offset in range(1, SHORT_LEN):
            grad_block = grad_block + weights[:, offset][:, None, :] * trailing[:, offset:offset + length]
        short_block = jnp.stack([jnp.sum(grads * padded[:, lag - offset:lag - offset + length], axis=1) for offset in range(SHORT_LEN)], axis=1)
        cross = jnp.fft.rfft(grad_long, fft_len, axis=0) * jnp.conj(jnp.fft.rfft(mixed, fft_len, axis=0))
        filt_block = jnp.fft.irfft(cross, fft_len, axis=0)[:FILTER_LEN]
        return grad_block.astype(jnp.bfloat16), filt_block.astype(jnp.float32), short_block.astype(jnp.float32)

    starts = (jnp.arange(blocks) * block).astype(jnp.int32)
    grad_all, filt_all, short_all = lax.map(one_block, starts)
    grad_inputs = jnp.moveaxis(grad_all, 0, 2).reshape(3, length, WIDTH)
    grad_filters = jnp.moveaxis(filt_all, 0, 1).reshape(FILTER_LEN, WIDTH)
    grad_short = jnp.moveaxis(short_all, 0, 2).reshape(3, SHORT_LEN, WIDTH)
    return grad_inputs, grad_filters, grad_short
```

```python
import functools

import jax
import jax.numpy as jnp
import numpy as np
from jax import lax
from jax.experimental import pallas as pl
from jax.experimental.pallas import tpu as pltpu
from jax.sharding import PartitionSpec as P

BF16 = jnp.bfloat16
F32 = jnp.float32


def dft_matrices(count):
    angle = np.arange(count)[None, :] * (np.arange(count // 2)[:, None] + 0.5) * (2 * np.pi / count)
    forward = np.concatenate([np.cos(angle), -np.sin(angle)], axis=0)
    backward = forward.T * (2.0 / count)
    return forward, backward


def split(matrix):
    high = matrix.astype(BF16)
    low = (matrix - high.astype(np.float64)).astype(BF16)
    return high, low


def dot(a, b):
    return jnp.dot(a, b, preferred_element_type=F32)


def forward(mat, signal):
    return dot(mat[0], signal) + dot(mat[1], signal)


def inverse(mat, spectrum):
    high = spectrum.astype(BF16)
    low = (spectrum - high.astype(F32)).astype(BF16)
    return dot(mat[0], high) + dot(mat[1], high) + dot(mat[0], low)


def times(a, b):
    half = a.shape[0] // 2
    ar, ai, br, bi = a[:half], a[half:], b[:half], b[half:]
    return jnp.concatenate([ar * br - ai * bi, ar * bi + ai * br], axis=0)


def times_conj(a, b):
    half = a.shape[0] // 2
    ar, ai, br, bi = a[:half], a[half:], b[:half], b[half:]
    return jnp.concatenate([ar * br + ai * bi, ai * br - ar * bi], axis=0)


def delayed(x, before):
    row = lax.broadcasted_iota(jnp.int32, x.shape, 0)
    older, newer = before[0:1], before[1:2]
    one = jnp.where(row == 0, newer, pltpu.roll(x, 1, 0))
    two = jnp.where(row == 0, older, jnp.where(row == 1, newer, pltpu.roll(x, 2, 0)))
    return x, one, two


def advanced(x):
    rows = x.shape[0]
    row = lax.broadcasted_iota(jnp.int32, x.shape, 0)
    one = jnp.where(row == rows - 1, 0.0, pltpu.roll(x, rows - 1, 0))
    two = jnp.where(row >= rows - 2, 0.0, pltpu.roll(x, rows - 2, 0))
    return x, one, two


def weighted(terms, weights, i):
    out = weights[i, 0:1] * terms[0]
    for j in range(1, len(terms)):
        out = out + weights[i, j : j + 1] * terms[j]
    return out


def tail_body(near_ref, last_ref, w_ref, out_ref):
    w = w_ref[...].astype(F32)
    lead = near_ref.shape[1]
    shorts = []
    for i in (1, 2):
        x = last_ref[i - 1].astype(F32)
        before = near_ref[i - 1].astype(F32)[lead - 2 :]
        shorts.append(weighted(delayed(x, before), w, i))
    out_ref[...] = (shorts[0] * shorts[1]).astype(BF16)


def local_body(x_ref, before_ref, go_ref, w_ref, taps_ref, fh_ref, fl_ref, head_ref, a_ref, g_ref, h_ref):
    w = w_ref[...].astype(F32)
    rows = go_ref.shape[0]
    reach = taps_ref.shape[0]
    q, k, v = [
        weighted(delayed(x_ref[i].astype(F32), before_ref[i].astype(F32)), w, i) for i in range(3)
    ]
    mixed = (k * v).astype(BF16)
    grad_long = (go_ref[...].astype(F32) * q).astype(BF16)
    head_ref[...] = grad_long[:reach]
    a_ref[...] = forward((fh_ref[:, reach:], fl_ref[:, reach:]), mixed)
    g_ref[...] = forward((fh_ref[:, :rows], fl_ref[:, :rows]), grad_long)
    h_ref[...] = forward((fh_ref[:, :reach], fl_ref[:, :reach]), taps_ref[...])


def filter_body(halo_ref, a_ref, g_ref, fh_ref, fl_ref, bh_ref, bl_ref, full_ref, out_ref):
    full = a_ref[...] + forward((fh_ref[...], fl_ref[...]), halo_ref[...])
    full_ref[...] = full
    out_ref[...] = inverse((bh_ref[...], bl_ref[...]), times_conj(full, g_ref[...]))


def output_body(
    x_ref, before_ref, go_ref, w_ref, next_ref, a_ref, g_ref, h_ref, fh_ref, fl_ref, bh_ref, bl_ref,
    gi_ref, tail_ref, first_ref, short_ref,
):
    w = w_ref[...].astype(F32)
    rows = go_ref.shape[0]
    reach = next_ref.shape[0]
    h = h_ref[...]
    long_out = inverse((bh_ref[reach:], bl_ref[reach:]), times(a_ref[...], h))
    g = g_ref[...] + forward((fh_ref[...], fl_ref[...]), next_ref[...])
    grad_mixed = inverse((bh_ref[:rows], bl_ref[:rows]), times_conj(g, h))
    shifted = [delayed(x_ref[i].astype(F32), before_ref[i].astype(F32)) for i in range(3)]
    k, v = weighted(shifted[1], w, 1), weighted(shifted[2], w, 2)
    grads = (go_ref[...].astype(F32) * long_out, grad_mixed * v, grad_mixed * k)
    for i in range(3):
        low = grads[i].astype(BF16)
        first_ref[i] = low[:2]
        wide = low.astype(F32)
        result = weighted(advanced(wide), w, i)
        tail_ref[i] = result[rows - 2 :]
        gi_ref[i] = result.astype(BF16)
        for j in range(3):
            short_ref[i, j : j + 1] = jnp.sum(wide * shifted[i][j], axis=0, keepdims=True)


def finish_body(old_ref, tail_ref, next_ref, w_ref, out_ref):
    w = w_ref[...].astype(F32)
    rows = old_ref.shape[1]
    row = lax.broadcasted_iota(jnp.int32, old_ref.shape[1:], 0)
    for i in range(3):
        after = next_ref[i].astype(F32)
        part = tail_ref[i]
        one = part[0:1] + w[i, 2:3] * after[0:1]
        two = part[1:2] + w[i, 1:2] * after[0:1] + w[i, 2:3] * after[1:2]
        old = old_ref[i].astype(F32)
        new = jnp.where(row == rows - 2, one, jnp.where(row == rows - 1, two, old))
        out_ref[i] = new.astype(BF16)


def exchange(block, axis, flip):
    return lax.ppermute(block, axis, [(i, i ^ flip) for i in range(lax.axis_size(axis))])


def shift(block, axis, distance):
    count = lax.axis_size(axis)
    return lax.ppermute(
        block, axis, [(i, i + distance) for i in range(count) if 0 <= i + distance < count]
    )


def pick(stacked, index):
    return lax.dynamic_index_in_dim(stacked, index, 0, keepdims=False)


def reduce_filters(terms, parts):
    seq, fsdp = lax.axis_size("seq"), lax.axis_size("fsdp")
    taps, channels = terms.shape
    if seq & (seq - 1) or fsdp & (fsdp - 1) or channels % (128 * seq) or seq < 2 or seq > 16:
        pieces = lax.all_to_all(terms, "fsdp", split_axis=0, concat_axis=1, tiled=True)
        return lax.psum(pieces, "seq")
    me, mine = lax.axis_index("seq"), lax.axis_index("fsdp")
    width = channels // seq
    pairs = seq // 2
    by_owner = terms.reshape(taps, pairs, 2, width).transpose(2, 1, 0, 3)
    side = me % 2
    keep, give = pick(by_owner, side), pick(by_owner, 1 - side)
    keep = keep + exchange(give.astype(BF16), "seq", 1).astype(F32)
    place = me // 2
    own = pick(keep, place)
    for flip in range(1, pairs):
        own = own + exchange(pick(keep, place ^ flip).astype(BF16), "seq", 2 * flip).astype(F32)
    blocks = own.astype(BF16).reshape(fsdp, taps // fsdp, width)
    wanted = jnp.zeros((fsdp, taps // fsdp, width), BF16)
    wanted = lax.dynamic_update_index_in_dim(wanted, pick(blocks, mine), mine, 0)
    for flip in range(1, fsdp):
        got = exchange(pick(blocks, mine ^ flip), "fsdp", flip)
        wanted = lax.dynamic_update_index_in_dim(wanted, got, mine ^ flip, 0)
    pieces = [wanted] + [exchange(wanted, "seq", 2 * flip) for flip in range(1, pairs)]
    others = [exchange(piece, "seq", 1) for piece in pieces]
    whole = jnp.zeros((seq, fsdp, taps // fsdp, width), BF16)
    for flip in range(pairs):
        whole = lax.dynamic_update_index_in_dim(whole, pieces[flip], me ^ (2 * flip), 0)
        whole = lax.dynamic_update_index_in_dim(whole, others[flip], me ^ (2 * flip) ^ 1, 0)
    return whole.transpose(2, 1, 0, 3).reshape(taps // fsdp, fsdp * channels).astype(F32)


def reduce_short(terms):
    seq = lax.axis_size("seq")
    if seq & (seq - 1):
        return lax.psum(terms, "seq")
    flip = 1
    while flip < seq:
        terms = terms + exchange(terms, "seq", flip)
        flip *= 2
    return terms


def local(inputs, grad_out, filters, short_weights):
    kinds, rows, channels = inputs.shape
    lag = short_weights.shape[1] - 1
    fsdp = lax.axis_size("fsdp")
    reach = filters.shape[0] * fsdp
    count = rows + reach
    fwd, bwd = dft_matrices(count)
    fh, fl = [jnp.asarray(m) for m in split(fwd)]
    bh, bl = [jnp.asarray(m) for m in split(bwd)]
    width = 256 if channels % 256 == 0 else channels
    grid = (channels // width,)
    near = 16

    def cols(*lead):
        return pl.BlockSpec((*lead, width), lambda c: (*([0] * len(lead)), c))

    def whole(shape):
        return pl.BlockSpec(shape, lambda c: (0, 0))

    def sds(shape, dtype):
        return jax.ShapeDtypeStruct(shape, dtype)

    w_spec = cols(kinds, lag + 1)
    before = shift(inputs[:, rows - lag :], "seq", 1)
    skip = rows - reach
    pair = inputs[1:]
    tail = pl.pallas_call(
        tail_body,
        grid=grid,
        in_specs=[
            pl.BlockSpec((2, near, width), lambda c: (0, skip // near - 1, c)),
            pl.BlockSpec((2, reach, width), lambda c: (0, skip // reach, c)),
            w_spec,
        ],
        out_specs=cols(reach),
        out_shape=sds((reach, channels), BF16),
        name="tail",
    )(pair, pair, short_weights)
    halo = shift(tail, "seq", 1)
    taps = lax.all_to_all(filters, "fsdp", split_axis=1, concat_axis=0, tiled=True)

    head, a_local, g_local, h = pl.pallas_call(
        local_body,
        grid=grid,
        in_specs=[cols(kinds, rows), cols(kinds, lag), cols(rows), w_spec, cols(reach)]
        + [whole((count, count))] * 2,
        out_specs=[cols(reach), cols(count), cols(count), cols(count)],
        out_shape=[sds((reach, channels), BF16)] + [sds((count, channels), F32)] * 3,
        name="local",
    )(inputs, before, grad_out, short_weights, taps, fh, fl)

    order = reach - np.arange(reach)
    a_full, terms = pl.pallas_call(
        filter_body,
        grid=grid,
        in_specs=[cols(reach), cols(count), cols(count)]
        + [whole((count, reach))] * 2
        + [whole((reach, count))] * 2,
        out_specs=[cols(count), cols(reach)],
        out_shape=[sds((count, channels), F32), sds((reach, channels), F32)],
        name="filters",
    )(halo, a_local, g_local, fh[:, :reach], fl[:, :reach], bh[order], bl[order])
    grad_filters = reduce_filters(terms, None)

    following = shift(head, "seq", -1)
    partial, tails, firsts, shorts = pl.pallas_call(
        output_body,
        grid=grid,
        in_specs=[
            cols(kinds, rows), cols(kinds, lag), cols(rows), w_spec, cols(reach),
            cols(count), cols(count), cols(count),
        ]
        + [whole((count, reach))] * 2
        + [whole((count, count))] * 2,
        out_specs=[cols(kinds, rows), cols(kinds, lag), cols(kinds, lag), cols(kinds, lag + 1)],
        out_shape=[
            sds((kinds, rows, channels), BF16),
            sds((kinds, lag, channels), F32),
            sds((kinds, lag, channels), BF16),
            sds((kinds, lag + 1, channels), F32),
        ],
        name="outputs",
    )(
        inputs, before, grad_out, short_weights, following, a_full, g_local, h,
        fh[:, rows:], fl[:, rows:], bh, bl,
    )
    grad_short = reduce_short(shorts)
    after = shift(firsts, "seq", -1)
    last = pl.BlockSpec((kinds, near, width), lambda c: (0, rows // near - 1, c))
    grad_inputs = pl.pallas_call(
        finish_body,
        grid=grid,
        in_specs=[last, cols(kinds, lag), cols(kinds, lag), w_spec],
        out_specs=last,
        out_shape=sds((kinds, rows, channels), BF16),
        input_output_aliases={0: 0},
        name="finish",
    )(partial, tails, after, short_weights)
    return (grad_inputs, grad_filters, grad_short)


def solution(mesh):
    placed = (P(None, "seq", "fsdp"), P("seq", "fsdp"), P("fsdp", None), P(None, None, "fsdp"))
    return jax.shard_map(
        local,
        mesh=mesh,
        in_specs=placed,
        out_specs=(P(None, "seq", "fsdp"), P("fsdp", None), P(None, None, "fsdp")),
        check_vma=False,
    )
```
